256 devices in a mesh: row: 16 (over z_hi, y), col: 16 (over z_lo, x, core).
Axes of the slice: x: 4, y: 4, z: 8 (z_hi: 4, z_lo: 2; z = z_hi * 2 + z_lo), core: 2. Of those that a mesh axis runs over, the one named last changes fastest.
Arguments:
- a11: float32 [256, 256], replicated, as said below
- linv11: float32 [256, 256], replicated, as said below
- a21: float32 [16384, 256], P(('row', 'col')), may hold values from -6 to 6
- l21: float32 [16384, 256], P(('row', 'col')), may hold values from -0.4 to 0.4
- a22: float32 [16384, 16384], P('row', 'col'), may hold values from -6 to 6
Outputs:
- diag_block: float32 [256, 256], replicated
- panel: float32 [16384, 256], P(('row', 'col'))
- trailing: float32 [16384, 16384], P('row', 'col')
The draws below stay inside these ranges and needn't reach their ends.
Inputs may be any that keep to these rules, and one draw needn't show every extreme that they name: `a11`: symmetric. `linv11`: lower triangular with a positive diagonal.
All inputs are finite; a program needn't handle non-finite values.
Results may differ from the reference program's by a relative error of at most 0.00005.
Values sent between devices are 32-bit elements; how exact they have to be, the bound alone decides.
A program may use at most 64 MiB of HBM per device.

```python
import jax
import jax.numpy as jnp
from jax import lax

NB = 256
M = 16384


def draw_a11(key, part):
    gauss = jax.random.normal(key, (NB, NB), jnp.float32)
    return (gauss + gauss.T) * 0.5


def draw_linv11(key, part):
    first = jax.random.fold_in(key, 11)
    second = jax.random.fold_in(key, 12)
    diagonal = jax.random.uniform(first, (NB,), jnp.float32, 0.5, 1.0)
    lower = jax.random.normal(second, (NB, NB), jnp.float32) * (0.5 / NB ** 0.5)
    rows = jnp.arange(NB)[:, None]
    cols = jnp.arange(NB)[None, :]
    strict = jnp.where(rows > cols, lower, 0.0)
    return strict + jnp.diag(diagonal)


def shard_levels(own_key, dims, shards, low, largest):
    gain = 1.0
    for dim, parts in shards:
        steps = jax.random.uniform(jax.random.fold_in(jax.random.fold_in(own_key, 6), dim), (parts,), jnp.float32, low / len(shards), largest / len(shards))
        gain = gain * jnp.repeat(jnp.exp(steps), dims[dim] // parts).reshape((-1,) + (1,) * (len(dims) - 1 - dim))
    return gain


def normal_values(stream_key, extent, width, reach, split=(), kind=jnp.bfloat16):
    values = jax.random.normal(stream_key, extent, jnp.float32) * width
    if len(split) > 0:
        values = shard_levels(stream_key, extent, split, -0.22, 0.18) * values
    return jnp.clip(values, min=-reach, max=reach).astype(kind)


def setup_inputs(seed: int = 0) -> dict:
    key_of = jax.random.split(jax.random.key(seed), 6)
    return {
        "a11": draw_a11(jax.random.fold_in(key_of[5], 71), 0),
        "linv11": draw_linv11(jax.random.fold_in(key_of[5], 71), 0),
        "a21": normal_values(key_of[2], (M, NB), 1.0, 6.0, ((0, 256),), jnp.float32),
        "l21": normal_values(key_of[3], (M, NB), 0.0625, 0.4, ((0, 256),), jnp.float32),
        "a22": normal_values(key_of[4], (M, M), 1.0, 6.0, ((0, 16), (1, 16)), jnp.float32),
    }


def mult(a, b):
    return jnp.dot(a, b, precision=lax.Precision.HIGHEST, preferred_element_type=jnp.float32)


def reference(a11, linv11, a21, l21, a22):
    diag_block = mult(mult(linv11, a11), linv11.T)
    correction = 0.5 * mult(l21, diag_block)
    half = mult(a21, linv11.T) - correction
    trailing = a22 - (mult(half, l21.T) + mult(l21, half.T))
    panel = half - correction
    return diag_block, panel, trailing
```

```python
import jax
import jax.numpy as jnp
from jax import lax
from jax.experimental import pallas as pl
from jax.experimental.pallas import tpu as pltpu
from jax.sharding import PartitionSpec as P

F32 = jnp.float32
BF16 = jnp.bfloat16
MESH = pl.DeviceIdType.MESH
A, L = 0, 1


def split(x):
    hi = x.astype(BF16)
    return hi, (x - hi.astype(F32)).astype(BF16)


def mult(a, b):
    return jnp.dot(a, b, precision=lax.Precision.HIGHEST, preferred_element_type=F32)


def nn(a, b):
    return jnp.dot(a, b, preferred_element_type=F32)


def nt(a, b):
    return lax.dot_general(a, b, (((1,), (1,)), ((), ())), preferred_element_type=F32)


def chunk_of(col, z, y):
    zp, yp, lop, xp = col // 4, col % 4, col // 8, (col // 2) % 4
    step = (z - zp + 4) % 4
    xj = (yp + 2 + xp - y + 4) % 4
    lo = (lop + 1 - step % 2) % 2
    return lo * 8 + xj * 2 + step // 2


def cell_of(panel, chunk):
    zp, yp, lop, xp = panel // 4, panel % 4, panel // 8, (panel // 2) % 4
    lo, xj, core = chunk // 8, (chunk // 2) % 4, chunk % 2
    step = 2 * core + 1 - (lo + lop) % 2
    return ((zp + step) % 4) * 4 + (yp + 2 - xj + xp + 4) % 4


def kernel(a11, linv, a21, l21, a22, diag_o, panel_o, out, row_a, row_l, col_a, col_l,
           r_hi, r_lo, w_hi, w_lo, big, send_sem, row_sem, col_sem, in_sem, out_sem):
    r = lax.axis_index("row")
    p = lax.axis_index("col")
    z, y = r // 4, r % 4
    lo, x, k = p // 8, (p // 2) % 4, p % 2
    rows = (row_a, row_l)
    cols = (col_a, col_l)
    own = (a21, l21)

    sib = (r, lo * 8 + x * 2 + (1 - k))
    par = (r, (1 - lo) * 8 + x * 2 + k)
    xu = (r, lo * 8 + ((x + 1) % 4) * 2 + k)
    xd = (r, lo * 8 + ((x + 3) % 4) * 2 + k)
    zu = (((z + 1) % 4) * 4 + y, p)
    zd = (((z + 3) % 4) * 4 + y, p)
    yu = (z * 4 + (y + 1) % 4, p)
    yd = (z * 4 + (y + 3) % 4, p)
    t_to = (cell_of(r, p), r)
    t_from = (p, chunk_of(p, z, y))

    barrier = pltpu.get_barrier_semaphore()
    for peer in (sib, par, xu, xd, zu, zd, yu, yd, t_to, t_from):
        pl.semaphore_signal(barrier, inc=1, device_id=peer, device_id_type=MESH)

    load = pltpu.make_async_copy(a22, big, in_sem)
    load.start()

    def row_slot(dl, dx, dk):
        return ((lo + dl) % 2) * 8 + ((x + dx) % 4) * 2 + (k + dk) % 2

    def col_slot(dz, dy):
        return chunk_of(p, (z + dz) % 4, (y + dy) % 4)

    def row_idx(dl, dx, dk, pc):
        return ((dl * 4 + dx) * 2 + dk) * 2 + pc

    def col_idx(dz, dy, pc):
        return (dz * 4 + dy) * 2 + pc

    started = []

    def send(src, dst, sem, peer):
        copy = pltpu.make_async_remote_copy(
            src_ref=src, dst_ref=dst, send_sem=send_sem.at[len(started)], recv_sem=sem,
            device_id=peer, device_id_type=MESH)
        copy.start()
        started.append(copy)

    def send_row(src, slot, pc, peer, dl, dx, dk):
        send(src, rows[pc].at[slot], row_sem.at[row_idx(dl, dx, dk, pc)], peer)

    def fwd_row(dl, dx, dk, pc, peer, there):
        slot = row_slot(dl, dx, dk)
        send_row(rows[pc].at[slot], slot, pc, peer, *there)

    def fwd_col(dz, dy, pc, peer, there):
        slot = col_slot(dz, dy)
        send(cols[pc].at[slot], cols[pc].at[slot], col_sem.at[col_idx(*there, pc)], peer)

    def got(ref, sem):
        pltpu.make_async_remote_copy(
            src_ref=ref, dst_ref=ref, send_sem=send_sem.at[0], recv_sem=sem,
            device_id=sib, device_id_type=MESH).wait_recv()

    def got_row(dl, dx, dk, pc):
        got(rows[pc].at[row_slot(dl, dx, dk)], row_sem.at[row_idx(dl, dx, dk, pc)])

    def got_col(dz, dy, pc):
        got(cols[pc].at[col_slot(dz, dy)], col_sem.at[col_idx(dz, dy, pc)])

    def to_sib(dl, dx, pc):
        fwd_row(dl, dx, 0, pc, sib, (dl, dx, 1))

    def col_out(dz):
        for pc in (A, L):
            fwd_col(dz, 0, pc, yu, (dz, 3))
            fwd_col(dz, 0, pc, yd, (dz, 1))

    def col_relay(dz):
        got_col(dz, 3, A)
        fwd_col(dz, 3, A, yu, (dz, 2))
        got_col(dz, 1, L)
        fwd_col(dz, 1, L, yd, (dz, 2))

    inv = linv[...]
    inv_t = inv.T
    diag = mult(mult(inv, a11[...]), inv_t)
    diag_o[...] = diag
    correction = 0.5 * mult(l21[...], diag)
    panel_o[...] = (mult(a21[...], inv_t) - correction) - correction
    for i, w in enumerate((inv, diag, inv_t)):
        hi, low = split(w)
        w_hi[:, 256 * i:256 * (i + 1)] = hi
        w_lo[:, 256 * i:256 * (i + 1)] = low
    row_a[p] = a21[...]
    row_l[p] = l21[...]

    pl.semaphore_wait(barrier, 10)

    for pc in (A, L):
        send(own[pc], cols[pc].at[p], col_sem.at[col_idx(0, 0, pc)], t_to)
    for pc in (A, L):
        send_row(own[pc], p, pc, par, 1, 0, 0)
        send_row(own[pc], p, pc, xu, 0, 3, 0)
        send_row(own[pc], p, pc, xd, 0, 1, 0)
        send_row(own[pc], p, pc, sib, 0, 0, 1)

    for pc in (A, L):
        got_row(1, 0, 0, pc)
        fwd_row(1, 0, 0, pc, xu, (1, 3, 0))
        fwd_row(1, 0, 0, pc, xd, (1, 1, 0))
        to_sib(1, 0, pc)
    got_row(0, 3, 0, A)
    fwd_row(0, 3, 0, A, xu, (0, 2, 0))
    got_row(0, 1, 0, L)
    fwd_row(0, 1, 0, L, xd, (0, 2, 0))
    got_row(0, 3, 0, L)
    got_row(0, 1, 0, A)
    for dx in (3, 1):
        for pc in (A, L):
            to_sib(0, dx, pc)

    for pc in (A, L):
        got_col(0, 0, pc)
        fwd_col(0, 0, pc, zu, (3, 0))
        fwd_col(0, 0, pc, zd, (1, 0))
        fwd_col(0, 0, pc, yu, (0, 3))
        fwd_col(0, 0, pc, yd, (0, 1))

    got_row(1, 3, 0, A)
    fwd_row(1, 3, 0, A, xu, (1, 2, 0))
    got_row(1, 1, 0, L)
    fwd_row(1, 1, 0, L, xd, (1, 2, 0))
    got_row(1, 3, 0, L)
    got_row(1, 1, 0, A)
    for dx in (3, 1):
        for pc in (A, L):
            to_sib(1, dx, pc)

    got_col(3, 0, A)
    fwd_col(3, 0, A, zu, (2, 0))
    got_col(1, 0, L)
    fwd_col(1, 0, L, zd, (2, 0))
    col_relay(0)
    got_col(3, 0, L)
    got_col(1, 0, A)
    col_out(3)
    col_out(1)

    for dl in (0, 1):
        for pc in (A, L):
            got_row(dl, 2, 0, pc)
            to_sib(dl, 2, pc)
    for dl in (0, 1):
        for dx in range(4):
            for pc in (A, L):
                got_row(dl, dx, 1, pc)

    @pl.loop(0, 16)
    def _(j):
        at = pl.ds(pl.multiple_of(j * 64, 64), 64)
        for pc in (A, L):
            hi, low = split(rows[pc][j])
            r_hi[at, 256 * pc:256 * (pc + 1)] = hi
            r_lo[at, 256 * pc:256 * (pc + 1)] = low

    for pc in (A, L):
        got_col(2, 0, pc)
    col_out(2)
    got_col(0, 3, L)
    got_col(0, 1, A)
    for pc in (A, L):
        got_col(0, 2, pc)
    col_relay(3)
    col_relay(1)
    load.wait()

    stores = []

    def update(pairs):
        l_c = jnp.concatenate([col_l[pl.ds(2 * i, 2)].reshape(128, 256) for i in pairs], axis=0)
        a_c = jnp.concatenate([col_a[pl.ds(2 * i, 2)].reshape(128, 256) for i in pairs], axis=0)
        l_hi, l_lo = split(l_c)
        a_hi, a_lo = split(a_c)
        both = nn(l_hi, w_hi[:, :512]) + nn(l_hi, w_lo[:, :512]) + nn(l_lo, w_hi[:, :512])
        right = nn(a_hi, w_hi[:, 512:]) + nn(a_hi, w_lo[:, 512:]) + nn(a_lo, w_hi[:, 512:])
        c = jnp.concatenate([both[:, :256], right - both[:, 256:]], axis=1)
        c_hi, c_lo = split(c)
        for m in range(4):
            at = slice(256 * m, 256 * (m + 1))
            u = nt(r_hi[at, :], c_hi) + nt(r_hi[at, :], c_lo) + nt(r_lo[at, :], c_hi)
            for n, i in enumerate(pairs):
                lanes = pl.ds(pl.multiple_of(i * 128, 128), 128)
                big[at, lanes] = big[at, lanes] - u[:, 128 * n:128 * (n + 1)]
        for i in pairs:
            lanes = pl.ds(pl.multiple_of(i * 128, 128), 128)
            copy = pltpu.make_async_copy(big.at[:, lanes], out.at[:, lanes], out_sem.at[len(stores)])
            copy.start()
            stores.append(copy)

    def pair(dz, dy):
        return col_slot(dz, dy) // 2

    for dz in (3, 1):
        got_col(dz, 3, L)
        got_col(dz, 1, A)
        for pc in (A, L):
            got_col(dz, 2, pc)
    update([pair(1, 0), pair(1, 1)])
    col_relay(2)
    update([pair(1, 2), pair(1, 3)])
    got_col(2, 3, L)
    got_col(2, 1, A)
    update([pair(0, 0), pair(0, 1)])
    for pc in (A, L):
        got_col(2, 2, pc)
    update([pair(0, 2), pair(0, 3)])

    for copy in started:
        copy.wait_send()
    for copy in stores:
        copy.wait()


def body(a11, linv11, a21, l21, a22):
    vmem = pl.BlockSpec(memory_space=pltpu.VMEM)
    anywhere = pl.BlockSpec(memory_space=pl.ANY)
    return pl.pallas_call(
        kernel,
        out_shape=(
            jax.ShapeDtypeStruct((256, 256), F32),
            jax.ShapeDtypeStruct((64, 256), F32),
            jax.ShapeDtypeStruct((1024, 1024), F32),
        ),
        in_specs=[vmem, vmem, vmem, vmem, anywhere],
        out_specs=(vmem, vmem, anywhere),
        scratch_shapes=[pltpu.VMEM((16, 64, 256), F32)] * 4
        + [pltpu.VMEM((1024, 512), BF16)] * 2
        + [pltpu.VMEM((256, 768), BF16)] * 2
        + [pltpu.VMEM((1024, 1024), F32)]
        + [
            pltpu.SemaphoreType.DMA((62,)),
            pltpu.SemaphoreType.DMA((32,)),
            pltpu.SemaphoreType.DMA((32,)),
            pltpu.SemaphoreType.DMA,
            pltpu.SemaphoreType.DMA((8,)),
        ],
        compiler_params=pltpu.CompilerParams(
            collective_id=0, has_side_effects=True, vmem_limit_bytes=40 * 2**20),
        name="panel_step",
    )(a11, linv11, a21, l21, a22)


def solution(mesh):
    panel_spec = P(("row", "col"), None)
    return jax.shard_map(
        body,
        mesh=mesh,
        in_specs=(P(), P(), panel_spec, panel_spec, P("row", "col")),
        out_specs=(P(), panel_spec, P("row", "col")),
        check_vma=False,
    )
```

```python
import jax
import jax.numpy as jnp
from jax import lax
from jax.experimental import pallas as pl
from jax.experimental.pallas import tpu as pltpu
from jax.sharding import PartitionSpec as P

F32 = jnp.float32
BF16 = jnp.bfloat16
MESH = pl.DeviceIdType.MESH
A, L = 0, 1


def split(x):
    hi = x.astype(BF16)
    return hi, (x - hi.astype(F32)).astype(BF16)


def mult(a, b):
    return jnp.dot(a, b, precision=lax.Precision.HIGHEST, preferred_element_type=F32)


def nn(a, b):
    return jnp.dot(a, b, preferred_element_type=F32)


def nt(a, b):
    return lax.dot_general(a, b, (((1,), (1,)), ((), ())), preferred_element_type=F32)


def chunk_of(col, z, y):
    zp, yp, lop, xp = col // 4, col % 4, col // 8, (col // 2) % 4
    step = (z - zp + 4) % 4
    xj = (yp + 2 + xp - y + 4) % 4
    lo = (lop + 1 - step % 2) % 2
    return lo * 8 + xj * 2 + step // 2


def cell_of(panel, chunk):
    zp, yp, lop, xp = panel // 4, panel % 4, panel // 8, (panel // 2) % 4
    lo, xj, core = chunk // 8, (chunk // 2) % 4, chunk % 2
    step = 2 * core + 1 - (lo + lop) % 2
    return ((zp + step) % 4) * 4 + (yp + 2 - xj + xp + 4) % 4


def subtract(new, old, r_hi, r_lo, c_hi, c_lo, pairs, m):
    at = slice(256 * m, 256 * (m + 1))
    u = nt(r_hi[at, :], c_hi) + nt(r_hi[at, :], c_lo) + nt(r_lo[at, :], c_hi)
    for n, i in enumerate(pairs):
        lanes = pl.ds(pl.multiple_of(i * 128, 128), 128)
        new[at, lanes] = old[at, lanes] - u[:, 128 * n:128 * (n + 1)]


def last_pairs():
    r, p = lax.axis_index("row"), lax.axis_index("col")
    z, y = r // 4, r % 4
    return [chunk_of(p, z, (y + dy) % 4) // 2 for dy in (2, 3)]


def finish(big, diag, panel, r_hi, r_lo, c_hi, c_lo, diag_o, panel_o, out, done, sem):
    r, p = lax.axis_index("row"), lax.axis_index("col")
    z, y = r // 4, r % 4
    copies = [
        pltpu.make_async_copy(diag, diag_o, sem.at[0]),
        pltpu.make_async_copy(panel, panel_o, sem.at[1]),
    ]
    for dz in (0, 1):
        for dy in range(4):
            if dz == 0 and dy >= 2:
                continue
            i = chunk_of(p, (z + dz) % 4, (y + dy) % 4) // 2
            lanes = pl.ds(pl.multiple_of(i * 128, 128), 128)
            copies.append(pltpu.make_async_copy(big.at[:, lanes], out.at[:, lanes], sem.at[len(copies)]))
    for copy in copies:
        copy.start()
    pairs = last_pairs()
    for m in range(4):
        at = slice(256 * m, 256 * (m + 1))
        u = nt(r_hi[at, :], c_hi[...]) + nt(r_hi[at, :], c_lo[...]) + nt(r_lo[at, :], c_hi[...])
        for n, i in enumerate(pairs):
            lanes = pl.ds(pl.multiple_of(i * 128, 128), 128)
            done[at, 128 * n:128 * (n + 1)] = big[at, lanes] - u[:, 128 * n:128 * (n + 1)]
            copy = pltpu.make_async_copy(
                done.at[at, 128 * n:128 * (n + 1)], out.at[at, lanes], sem.at[len(copies)])
            copy.start()
            copies.append(copy)
    for copy in copies:
        copy.wait()


def kernel(a11_h, linv_h, a21_h, l21_h, a22, diag_o, panel_o, big, r_hi, r_lo, c_hi, c_lo,
           a11, linv, a21, l21, row_a, row_l, col_a, col_l, w_hi, w_lo,
           send_sem, row_sem, col_sem, in_sem):
    r = lax.axis_index("row")
    p = lax.axis_index("col")
    z, y = r // 4, r % 4
    lo, x, k = p // 8, (p // 2) % 4, p % 2
    rows = (row_a, row_l)
    cols = (col_a, col_l)
    own = (a21, l21)

    sib = (r, lo * 8 + x * 2 + (1 - k))
    par = (r, (1 - lo) * 8 + x * 2 + k)
    xu = (r, lo * 8 + ((x + 1) % 4) * 2 + k)
    xd = (r, lo * 8 + ((x + 3) % 4) * 2 + k)
    zu = (((z + 1) % 4) * 4 + y, p)
    zd = (((z + 3) % 4) * 4 + y, p)
    yu = (z * 4 + (y + 1) % 4, p)
    yd = (z * 4 + (y + 3) % 4, p)
    t_to = (cell_of(r, p), r)
    t_from = (p, chunk_of(p, z, y))

    barrier = pltpu.get_barrier_semaphore()
    for peer in (sib, par, xu, xd, zu, zd, yu, yd, t_to, t_from):
        pl.semaphore_signal(barrier, inc=1, device_id=peer, device_id_type=MESH)

    loads = [
        pltpu.make_async_copy(src, dst, in_sem.at[i])
        for i, (src, dst) in enumerate(
            ((a21_h, a21), (l21_h, l21), (linv_h, linv), (a11_h, a11), (a22, big)))
    ]
    for copy in loads:
        copy.start()

    def row_slot(dl, dx, dk):
        return ((lo + dl) % 2) * 8 + ((x + dx) % 4) * 2 + (k + dk) % 2

    def col_slot(dz, dy):
        return chunk_of(p, (z + dz) % 4, (y + dy) % 4)

    def row_idx(dl, dx, dk, pc):
        return ((dl * 4 + dx) * 2 + dk) * 2 + pc

    def col_idx(dz, dy, pc):
        return (dz * 4 + dy) * 2 + pc

    started = []

    def send(src, dst, sem, peer):
        copy = pltpu.make_async_remote_copy(
            src_ref=src, dst_ref=dst, send_sem=send_sem.at[len(started)], recv_sem=sem,
            device_id=peer, device_id_type=MESH)
        copy.start()
        started.append(copy)

    def send_row(src, slot, pc, peer, dl, dx, dk):
        send(src, rows[pc].at[slot], row_sem.at[row_idx(dl, dx, dk, pc)], peer)

    def fwd_row(dl, dx, dk, pc, peer, there):
        slot = row_slot(dl, dx, dk)
        send_row(rows[pc].at[slot], slot, pc, peer, *there)

    def fwd_col(dz, dy, pc, peer, there):
        slot = col_slot(dz, dy)
        send(cols[pc].at[slot], cols[pc].at[slot], col_sem.at[col_idx(*there, pc)], peer)

    def got(ref, sem):
        pltpu.make_async_remote_copy(
            src_ref=ref, dst_ref=ref, send_sem=send_sem.at[0], recv_sem=sem,
            device_id=sib, device_id_type=MESH).wait_recv()

    def got_row(dl, dx, dk, pc):
        got(rows[pc].at[row_slot(dl, dx, dk)], row_sem.at[row_idx(dl, dx, dk, pc)])

    def got_col(dz, dy, pc):
        got(cols[pc].at[col_slot(dz, dy)], col_sem.at[col_idx(dz, dy, pc)])

    def to_sib(dl, dx, pc):
        fwd_row(dl, dx, 0, pc, sib, (dl, dx, 1))

    def col_out(dz):
        for pc in (A, L):
            fwd_col(dz, 0, pc, yu, (dz, 3))
            fwd_col(dz, 0, 1 - pc, yd, (dz, 1))

    def col_relay(dz):
        got_col(dz, 3, A)
        fwd_col(dz, 3, A, yu, (dz, 2))
        got_col(dz, 1, L)
        fwd_col(dz, 1, L, yd, (dz, 2))

    for copy in loads[:4]:
        copy.wait()
    inv = linv[...]
    inv_t = inv.T
    diag = mult(mult(inv, a11[...]), inv_t)
    diag_o[...] = diag
    correction = 0.5 * mult(l21[...], diag)
    panel_o[...] = (mult(a21[...], inv_t) - correction) - correction
    for i, w in enumerate((inv, diag, inv_t)):
        hi, low = split(w)
        w_hi[:, 256 * i:256 * (i + 1)] = hi
        w_lo[:, 256 * i:256 * (i + 1)] = low
    row_a[p] = a21[...]
    row_l[p] = l21[...]

    pl.semaphore_wait(barrier, 10)

    for pc in (A, L):
        send(own[pc], cols[pc].at[p], col_sem.at[col_idx(0, 0, pc)], t_to)
    for pc in (A, L):
        send_row(own[pc], p, pc, par, 1, 0, 0)
        send_row(own[pc], p, pc, xu, 0, 3, 0)
        send_row(own[1 - pc], p, 1 - pc, xd, 0, 1, 0)
        send_row(own[pc], p, pc, sib, 0, 0, 1)

    for pc in (A, L):
        got_row(1, 0, 0, pc)
    for pc in (A, L):
        fwd_row(1, 0, 0, pc, xu, (1, 3, 0))
        fwd_row(1, 0, 0, 1 - pc, xd, (1, 1, 0))
        to_sib(1, 0, pc)
    got_row(0, 3, 0, A)
    fwd_row(0, 3, 0, A, xu, (0, 2, 0))
    got_row(0, 1, 0, L)
    fwd_row(0, 1, 0, L, xd, (0, 2, 0))
    got_row(0, 3, 0, L)
    got_row(0, 1, 0, A)
    for dx in (3, 1):
        for pc in (A, L):
            to_sib(0, dx, pc)

    got_col(0, 0, A)
    fwd_col(0, 0, A, zu, (3, 0))
    fwd_col(0, 0, A, yu, (0, 3))
    got_col(0, 0, L)
    fwd_col(0, 0, L, zd, (1, 0))
    fwd_col(0, 0, L, yd, (0, 1))
    fwd_col(0, 0, L, zu, (3, 0))
    fwd_col(0, 0, A, zd, (1, 0))
    fwd_col(0, 0, L, yu, (0, 3))
    fwd_col(0, 0, A, yd, (0, 1))

    got_row(1, 3, 0, A)
    fwd_row(1, 3, 0, A, xu, (1, 2, 0))
    got_row(1, 1, 0, L)
    fwd_row(1, 1, 0, L, xd, (1, 2, 0))
    got_row(1, 3, 0, L)
    got_row(1, 1, 0, A)
    for dx in (3, 1):
        for pc in (A, L):
            to_sib(1, dx, pc)

    got_col(3, 0, A)
    fwd_col(3, 0, A, zu, (2, 0))
    got_col(1, 0, L)
    fwd_col(1, 0, L, zd, (2, 0))
    col_relay(0)
    got_col(3, 0, L)
    got_col(1, 0, A)
    col_out(3)
    col_out(1)

    for dl in (0, 1):
        for pc in (A, L):
            got_row(dl, 2, 0, pc)
            to_sib(dl, 2, pc)
    for dl in (0, 1):
        for dx in range(4):
            for pc in (A, L):
                got_row(dl, dx, 1, pc)

    @pl.loop(0, 16)
    def _(j):
        at = pl.ds(pl.multiple_of(j * 64, 64), 64)
        for pc in (A, L):
            hi, low = split(rows[pc][j])
            r_hi[at, 256 * pc:256 * (pc + 1)] = hi
            r_lo[at, 256 * pc:256 * (pc + 1)] = low

    for pc in (A, L):
        got_col(2, 0, pc)
    col_out(2)
    got_col(0, 3, L)
    got_col(0, 1, A)
    for pc in (A, L):
        got_col(0, 2, pc)
    col_relay(3)
    col_relay(1)
    loads[4].wait()

    def operand(pairs):
        l_c = jnp.concatenate([col_l[pl.ds(2 * i, 2)].reshape(128, 256) for i in pairs], axis=0)
        a_c = jnp.concatenate([col_a[pl.ds(2 * i, 2)].reshape(128, 256) for i in pairs], axis=0)
        l_hi, l_lo = split(l_c)
        a_hi, a_lo = split(a_c)
        both = nn(l_hi, w_hi[:, :512]) + nn(l_hi, w_lo[:, :512]) + nn(l_lo, w_hi[:, :512])
        right = nn(a_hi, w_hi[:, 512:]) + nn(a_hi, w_lo[:, 512:]) + nn(a_lo, w_hi[:, 512:])
        return split(jnp.concatenate([both[:, :256], right - both[:, 256:]], axis=1))

    def update(pairs):
        hi, low = operand(pairs)
        for m in range(4):
            subtract(big, big, r_hi, r_lo, hi, low, pairs, m)

    def pair(dz, dy):
        return col_slot(dz, dy) // 2

    for dz in (3, 1):
        got_col(dz, 3, L)
        got_col(dz, 1, A)
        for pc in (A, L):
            got_col(dz, 2, pc)
    update([pair(1, 0), pair(1, 1)])
    col_relay(2)
    update([pair(1, 2), pair(1, 3)])
    got_col(2, 3, L)
    got_col(2, 1, A)
    update([pair(0, 0), pair(0, 1)])
    for pc in (A, L):
        got_col(2, 2, pc)
    hi, low = operand(last_pairs())
    c_hi[...] = hi
    c_lo[...] = low

    for copy in started:
        copy.wait_send()


def body(a11, linv11, a21, l21, a22):
    vmem = pl.BlockSpec(memory_space=pltpu.VMEM)
    hbm = pl.BlockSpec(memory_space=pltpu.HBM)
    shape = jax.ShapeDtypeStruct
    square, tall, whole = shape((256, 256), F32), shape((64, 256), F32), shape((1024, 1024), F32)
    diag, panel, big, r_hi, r_lo, c_hi, c_lo = pl.pallas_call(
        kernel,
        out_shape=(square, tall, whole)
        + (shape((1024, 512), BF16),) * 2
        + (shape((256, 512), BF16),) * 2,
        in_specs=[hbm] * 5,
        out_specs=(vmem,) * 7,
        scratch_shapes=[pltpu.VMEM((256, 256), F32)] * 2
        + [pltpu.VMEM((64, 256), F32)] * 2
        + [pltpu.VMEM((16, 64, 256), F32)] * 4
        + [pltpu.VMEM((256, 768), BF16)] * 2
        + [
            pltpu.SemaphoreType.DMA((62,)),
            pltpu.SemaphoreType.DMA((32,)),
            pltpu.SemaphoreType.DMA((32,)),
            pltpu.SemaphoreType.DMA((5,)),
        ],
        compiler_params=pltpu.CompilerParams(
            collective_id=0, has_side_effects=True, vmem_limit_bytes=30 * 2**20),
        name="panel_step",
    )(*(pltpu.with_memory_space_constraint(v, pltpu.HBM) for v in (a11, linv11, a21, l21, a22)))
    diag, panel, trailing = pl.pallas_call(
        finish,
        out_shape=(square, tall, whole),
        in_specs=[vmem] * 7,
        out_specs=(hbm,) * 3,
        scratch_shapes=[pltpu.VMEM((1024, 256), F32), pltpu.SemaphoreType.DMA((16,))],
        compiler_params=pltpu.CompilerParams(vmem_limit_bytes=30 * 2**20),
        name="last_columns",
    )(big, diag, panel, r_hi, r_lo, c_hi, c_lo)
    return diag, panel, trailing


def solution(mesh):
    panel_spec = P(("row", "col"), None)
    return jax.shard_map(
        body,
        mesh=mesh,
        in_specs=(P(), P(), panel_spec, panel_spec, P("row", "col")),
        out_specs=(P(), panel_spec, P("row", "col")),
        check_vma=False,
    )
```
